32 devices in a mesh: dp: 4 (over x, core), expert: 8 (over z, y).
Axes of the slice: x: 2, y: 2, z: 4, core: 2. Of those that a mesh axis runs over, the one named last changes fastest.
Arguments:
- tokens: bfloat16 [4096, 4096], P(('dp', 'expert')), may hold values from -6 to 6
- router: bfloat16 [4096, 8], replicated, may hold values from -0.09375 to 0.09375
- price: float32 [8], replicated, may hold values from -1 to 1
- w_in: bfloat16 [8, 4096, 8192], P('expert', None, 'dp'), may hold values from -0.09375 to 0.09375
- w_out: bfloat16 [8, 8192, 4096], P('expert', 'dp'), may hold values from -0.0625 to 0.0625
- assign: int32 [4096], P(('dp', 'expert')), may hold values from 0 to 7, as said below
Outputs:
- mixed: bfloat16 [4096, 4096], P(('dp', 'expert'))
- new_price: float32 [8], replicated
The draws below stay inside these ranges and needn't reach their ends.
Inputs may be any that keep to these rules, and one draw needn't show every extreme that they name: `assign`: every expert is named by exactly 512 tokens in all, and by at most 24 of the 128 tokens of one device (aligned blocks of 128 rows); on every device some expert is named exactly 24 times, and the experts' loads on one device are, in some order, the same 8 numbers on every device.
All inputs are finite; a program needn't handle non-finite values.
Results may differ from the reference program's by a relative error of at most 0.013.
Values may be sent and summed in bfloat16 or wider, within the bound.
A program may use at most 128 MiB of HBM per device.

```python
import jax
import jax.numpy as jnp
from jax import lax

D = 4096
FFW = 8192
TOK_DEV = 128
EXPERTS = 8
TOKENS = 4096
FF_DEV = 2048


def expert_labels(key):
    blocks = TOKENS // TOK_DEV
    half = EXPERTS // 2
    mean_load = TOK_DEV // EXPERTS
    which = jnp.arange(EXPERTS, dtype=jnp.int32)
    mirror = jnp.minimum(which, EXPERTS - 1 - which)
    lift = mean_load // 2 * (half - mirror) // half
    base = jnp.where(which < half, mean_load + lift, mean_load - lift).astype(jnp.int32)
    group_count = blocks // EXPERTS
    group_keys = jax.random.split(jax.random.fold_in(key, 11), group_count)
    perms = jax.vmap(lambda sub: jax.random.permutation(sub, EXPERTS))(group_keys).astype(jnp.int32)
    block_ids = jnp.arange(blocks, dtype=jnp.int32)
    shifts = perms[block_ids // EXPERTS]
    counts = base[(shifts + block_ids[:, None]) % EXPERTS]

    def one_block(count_row, sub):
        labels = jnp.repeat(jnp.arange(EXPERTS, dtype=jnp.int32), count_row, total_repeat_length=TOK_DEV)
        return jax.random.permutation(sub, labels)
    block_keys = jax.random.split(jax.random.fold_in(key, 23), blocks)
    return jax.vmap(one_block)(counts, block_keys).astype(jnp.int32)


def draw_assign(key, part):
    return expert_labels(key).reshape(TOKENS)


def level_of(key, dims, shards, smallest, largest):
    factor_of = 1.0
    for position, shards_of in shards:
        draws = jax.random.uniform(jax.random.fold_in(jax.random.fold_in(key, 6), position), (shards_of,), jnp.float32, smallest / len(shards), largest / len(shards))
        factor_of = factor_of * jnp.repeat(jnp.exp(draws), dims[position] // shards_of).reshape((-1,) + (1,) * (len(dims) - 1 - position))
    return factor_of


def gaussian(stream_key, dims, deviation, reach, cuts=(), held_as=jnp.bfloat16):
    level = level_of(stream_key, dims, cuts, -0.22, 0.18) if cuts else 1.0
    drawn = jax.random.normal(stream_key, dims, jnp.float32) * deviation * level
    return jnp.minimum(jnp.maximum(drawn, -reach), reach).astype(held_as)


def setup_inputs(seed: int = 0) -> dict:
    arg_keys = jax.random.split(jax.random.key(seed), 7)
    return {
        "tokens": gaussian(arg_keys[0], (TOKENS, D), 1.0, 6.0, ((0, 32),)),
        "router": gaussian(arg_keys[1], (D, EXPERTS), D ** -0.5, 0.09375),
        "price": jnp.clip(jax.random.uniform(arg_keys[2], (EXPERTS,), jnp.float32, -1.0, 1.0), -1.0, 1.0),
        "w_in": gaussian(arg_keys[3], (EXPERTS, D, FFW), D ** -0.5, 0.09375, ((0, 8), (2, 4))),
        "w_out": gaussian(arg_keys[4], (EXPERTS, FFW, D), FFW ** -0.5, 0.0625, ((0, 8), (1, 4))),
        "assign": draw_assign(jax.random.fold_in(arg_keys[6], 71), 0),
    }


BID_STEP = 0.01


def reference(tokens, router, price, w_in, w_out, assign):
    affinity = jnp.dot(tokens, router, preferred_element_type=jnp.float32)
    onehot = assign[:, None] == jnp.arange(EXPERTS, dtype=jnp.int32)[None, :]
    own = jnp.sum(jnp.where(onehot, affinity, 0.0), axis=1)
    rival = jnp.max(jnp.where(onehot, -1e30, affinity - price[None, :]), axis=1)
    bid = own - rival + BID_STEP
    new_price = jnp.max(jnp.where(onehot, bid[:, None], -1e30), axis=0)
    per_expert = TOKENS // EXPERTS
    order = jnp.argsort(assign, stable=True).astype(jnp.int32)
    groups = order.reshape(EXPERTS, per_expert)

    def run_expert(packed):
        index, first, second = packed
        rows = tokens[index].astype(jnp.float32)
        hidden = jax.nn.gelu(jnp.dot(rows, first.astype(jnp.float32)), approximate=True).astype(jnp.bfloat16)
        total = jnp.zeros((per_expert, D), jnp.float32)
        for block in range(FFW // FF_DEV):
            low = block * FF_DEV
            part = jnp.dot(hidden[:, low:low + FF_DEV].astype(jnp.float32), second[low:low + FF_DEV].astype(jnp.float32))
            part = lax.optimization_barrier(part.astype(jnp.bfloat16))
            total = total + part.astype(jnp.float32)
        return total.astype(jnp.bfloat16)

    outputs = lax.map(run_expert, (groups, w_in, w_out))
    expert_out = jnp.zeros((TOKENS, D), outputs.dtype).at[groups.reshape(-1)].set(outputs.reshape(-1, D))
    gate = jax.nn.sigmoid(own)
    mixed = (gate[:, None] * expert_out.astype(jnp.float32)).astype(jnp.bfloat16)
    return mixed, new_price
```

```python
import jax
import jax.numpy as jnp
from jax import lax
from jax.sharding import PartitionSpec as P

BID_STEP = 0.01


def shards(tokens, router, price, w_in, w_out, assign):
    experts = router.shape[1]
    width = tokens.shape[1]
    local_tokens = tokens.shape[0]
    capacity = 3 * local_tokens // (2 * experts)
    first = w_in[0]
    second = w_out[0]
    affinity = jnp.dot(tokens, router, preferred_element_type=jnp.float32)
    onehot = assign[:, None] == jnp.arange(experts, dtype=jnp.int32)[None, :]
    own = jnp.sum(jnp.where(onehot, affinity, 0.0), axis=1)
    rival = jnp.max(jnp.where(onehot, -1e30, affinity - price[None, :]), axis=1)
    bid = own - rival + BID_STEP
    local_best = jnp.max(jnp.where(onehot, bid[:, None], -1e30), axis=0)
    new_price = lax.pmax(local_best, ("dp", "expert"))
    lower = (jnp.arange(local_tokens)[:, None] >= jnp.arange(local_tokens)[None, :]).astype(jnp.bfloat16)
    running = jnp.dot(lower, onehot.astype(jnp.bfloat16), preferred_element_type=jnp.float32)
    slots = jnp.sum(jnp.where(onehot, running, 0.0), axis=1).astype(jnp.int32) - 1
    place = assign * capacity + slots
    pack = (place[None, :] == jnp.arange(experts * capacity, dtype=jnp.int32)[:, None]).astype(jnp.bfloat16)
    packed = jnp.dot(pack, tokens, preferred_element_type=jnp.float32).astype(jnp.bfloat16)
    mine = lax.all_to_all(packed.reshape(experts, capacity, width), "expert", split_axis=0, concat_axis=0, tiled=True)
    rows = lax.all_gather(mine.reshape(experts * capacity, width), "dp", axis=0, tiled=True)
    raw = jnp.dot(rows, first, preferred_element_type=jnp.float32)
    hidden = jax.nn.gelu(raw, approximate=True).astype(jnp.bfloat16)
    partial = jnp.dot(hidden, second, preferred_element_type=jnp.float32).astype(jnp.bfloat16)
    summed = lax.psum_scatter(partial, "dp", scatter_dimension=0, tiled=True)
    returned = lax.all_to_all(
        summed.reshape(experts, capacity, width), "expert", split_axis=0, concat_axis=0, tiled=True
    ).reshape(experts * capacity, width)
    picked = lax.dot_general(pack, returned, (((0,), (0,)), ((), ())), preferred_element_type=jnp.float32)
    gate = jax.nn.sigmoid(own)
    mixed = (gate[:, None] * picked).astype(jnp.bfloat16)
    return (mixed, new_price)


def solution(mesh):
    return jax.shard_map(
        shards,
        mesh=mesh,
        in_specs=(
            P(("dp", "expert"), None),
            P(),
            P(),
            P("expert", None, "dp"),
            P("expert", "dp", None),
            P(("dp", "expert")),
        ),
        out_specs=(P(("dp", "expert"), None), P()),
        check_vma=False,
    )
```

```python
import functools

import jax
import jax.numpy as jnp
from jax import lax
from jax.experimental import pallas as pl
from jax.experimental.pallas import tpu as pltpu
from jax.sharding import PartitionSpec as P

BID_STEP = 0.01
MESH = pl.DeviceIdType.MESH


def remote(src, dst, send, recv, a, b):
    return pltpu.make_async_remote_copy(
        src_ref=src, dst_ref=dst, send_sem=send, recv_sem=recv, device_id=(a, b), device_id_type=MESH
    )


def greet(dps, experts, a, b):
    barrier = pltpu.get_barrier_semaphore()
    for k in range(1, experts):
        pl.semaphore_signal(barrier, inc=1, device_id=(a, lax.rem(b + k, experts)), device_id_type=MESH)
    for k in range(1, dps):
        pl.semaphore_signal(barrier, inc=1, device_id=(lax.rem(a + k, dps), b), device_id_type=MESH)
    pl.semaphore_wait(barrier, experts + dps - 2)


def dispatch_kernel(dps, experts, packed, best, rows, bests, own_sem, s1, r1, s2, r2, s3, r3, sb, rb):
    a, b = lax.axis_index("dp"), lax.axis_index("expert")
    nx = dps // 2
    x, c = a // 2, lax.rem(a, 2)
    other = 2 * x + 1 - c
    greet(dps, experts, a, b)
    own = pltpu.make_async_copy(packed.at[b], rows.at[a, b], own_sem.at[0])
    own_best = pltpu.make_async_copy(best, bests.at[b], own_sem.at[1])
    own.start()
    own_best.start()

    def out(k):
        e = lax.rem(b + k, experts)
        return remote(packed.at[e], rows.at[a, b], s1.at[k], r1.at[k], a, e)

    def out_best(k):
        e = lax.rem(b + k, experts)
        return remote(best, bests.at[b], sb.at[k], rb.at[k], a, e)

    def source(k):
        return lax.rem(b + experts - k, experts)

    def across(q, k):
        to = 2 * lax.rem(x + q, nx) + c
        s = source(k)
        return remote(rows.at[a, s], rows.at[a, s], s2.at[q - 1, k], r2.at[q - 1, k], to, b)

    def beside(q, k):
        row = 2 * lax.rem(x + nx - q, nx) + c
        s = source(k)
        return remote(rows.at[row, s], rows.at[row, s], s3.at[q, k], r3.at[q, k], other, b)

    for k in range(1, experts):
        out(k).start()
    for k in range(1, experts):
        out_best(k).start()
    for k in range(experts):
        s = source(k)
        if k == 0:
            own.wait()
        else:
            remote(packed.at[s], rows.at[a, s], s1.at[k], r1.at[k], a, s).wait_recv()
        for q in range(1, nx):
            across(q, k).start()
        beside(0, k).start()
    for k in range(experts):
        s = source(k)
        for q in range(1, nx):
            row = 2 * lax.rem(x + nx - q, nx) + c
            remote(rows.at[row, s], rows.at[row, s], s2.at[q - 1, k], r2.at[q - 1, k], row, b).wait_recv()
            beside(q, k).start()
    for k in range(experts):
        s = source(k)
        for q in range(nx):
            row = 2 * lax.rem(x + nx - q, nx) + 1 - c
            remote(rows.at[row, s], rows.at[row, s], s3.at[q, k], r3.at[q, k], other, b).wait_recv()
    own_best.wait()
    for k in range(1, experts):
        s = source(k)
        remote(best, bests.at[s], sb.at[k], rb.at[k], a, s).wait_recv()
        out_best(k).wait_send()
        out(k).wait_send()
    for k in range(experts):
        for q in range(1, nx):
            across(q, k).wait_send()
        for q in range(nx):
            beside(q, k).wait_send()


def dispatch(packed, best, dps):
    experts, capacity, width = packed.shape
    nx = dps // 2
    sem = pltpu.SemaphoreType.DMA
    return pl.pallas_call(
        functools.partial(dispatch_kernel, dps, experts),
        out_shape=(
            jax.ShapeDtypeStruct((dps, experts, capacity, width), packed.dtype),
            jax.ShapeDtypeStruct((experts,) + best.shape, best.dtype),
        ),
        in_specs=[pl.BlockSpec(memory_space=pl.ANY)] * 2,
        out_specs=(pl.BlockSpec(memory_space=pl.ANY),) * 2,
        scratch_shapes=[
            sem((2,)),
            sem((experts,)),
            sem((experts,)),
            sem((nx - 1, experts)),
            sem((nx - 1, experts)),
            sem((nx, experts)),
            sem((nx, experts)),
            sem((experts,)),
            sem((experts,)),
        ],
        compiler_params=pltpu.CompilerParams(collective_id=0, has_side_effects=True),
        name="dispatch",
    )(packed, best)


def collect_kernel(
    dps, experts, part, best, back, bests, pair, far, final, own_sem, s1, r1, s2, r2, s3, r3, sb, rb
):
    a, b = lax.axis_index("dp"), lax.axis_index("expert")
    nx = dps // 2
    x, c = a // 2, lax.rem(a, 2)
    other = 2 * x + 1 - c
    width = part.shape[3]
    piece = width // 4
    greet(dps, experts, a, b)
    own_best = pltpu.make_async_copy(best, bests.at[a], own_sem.at[1])
    own_best.start()
    own = pltpu.make_async_copy(final.at[b], back.at[b], own_sem.at[0])

    def dest(k):
        return lax.rem(b + k, experts)

    def beside(q, k):
        s = dest(k)
        return remote(
            part.at[2 * lax.rem(x + q, nx) + 1 - c, s], pair.at[q, s], s1.at[q, k], r1.at[q, k], other, b
        )

    def across(q, k):
        s = dest(k)
        to = 2 * lax.rem(x + q, nx) + c
        return remote(pair.at[q, s], far.at[q - 1, s], s2.at[q - 1, k], r2.at[q - 1, k], to, b)

    def home(k):
        s = dest(k)
        return remote(final.at[s], back.at[b], s3.at[k], r3.at[k], a, s)

    def out_best(k):
        return remote(best, bests.at[a], sb.at[k], rb.at[k], lax.rem(a + k, dps), b)

    order = list(range(1, experts)) + [0]
    for k in order:
        for q in range(1, nx):
            beside(q, k).start()
    for k in order:
        beside(0, k).start()
    for k in range(1, dps):
        out_best(k).start()
    for k in order:
        s = dest(k)
        for q in range(1, nx):
            row = 2 * lax.rem(x + q, nx) + c
            beside(q, k).wait_recv()
            for p in range(4):
                cols = pl.ds(p * piece, piece)
                total = part[row, s, :, cols].astype(jnp.float32) + pair[q, s, :, cols].astype(jnp.float32)
                pair[q, s, :, cols] = total.astype(jnp.bfloat16)
            across(q, k).start()
    for k in order:
        s = dest(k)
        beside(0, k).wait_recv()
        for q in range(1, nx):
            across(q, k).wait_recv()
        for p in range(4):
            cols = pl.ds(p * piece, piece)
            total = part[a, s, :, cols].astype(jnp.float32) + pair[0, s, :, cols].astype(jnp.float32)
            for q in range(1, nx):
                total = total + far[q - 1, s, :, cols].astype(jnp.float32)
            final[s, :, cols] = total.astype(jnp.bfloat16)
        if k == 0:
            own.start()
        else:
            home(k).start()
    own.wait()
    own_best.wait()
    for k in range(1, dps):
        s = lax.rem(a + dps - k, dps)
        remote(best, bests.at[s], sb.at[k], rb.at[k], s, b).wait_recv()
        out_best(k).wait_send()
    for k in range(1, experts):
        s = lax.rem(b + experts - k, experts)
        remote(final.at[s], back.at[s], s3.at[k], r3.at[k], a, s).wait_recv()
        home(k).wait_send()
    for k in range(experts):
        for q in range(nx):
            beside(q, k).wait_send()
        for q in range(1, nx):
            across(q, k).wait_send()


def collect(part, best):
    dps, experts, capacity, width = part.shape
    nx = dps // 2
    sem = pltpu.SemaphoreType.DMA
    return pl.pallas_call(
        functools.partial(collect_kernel, dps, experts),
        out_shape=(
            jax.ShapeDtypeStruct((experts, capacity, width), part.dtype),
            jax.ShapeDtypeStruct((dps,) + best.shape, best.dtype),
        ),
        in_specs=[pl.BlockSpec(memory_space=pltpu.VMEM), pl.BlockSpec(memory_space=pl.ANY)],
        out_specs=(pl.BlockSpec(memory_space=pl.ANY),) * 2,
        scratch_shapes=[
            pltpu.VMEM((nx, experts, capacity, width), part.dtype),
            pltpu.VMEM((nx - 1, experts, capacity, width), part.dtype),
            pltpu.VMEM((experts, capacity, width), part.dtype),
            sem((2,)),
            sem((nx, experts)),
            sem((nx, experts)),
            sem((nx - 1, experts)),
            sem((nx - 1, experts)),
            sem((experts,)),
            sem((experts,)),
            sem((dps,)),
            sem((dps,)),
        ],
        compiler_params=pltpu.CompilerParams(
            collective_id=1, has_side_effects=True, vmem_limit_bytes=60 * 1024 * 1024
        ),
        name="collect",
    )(part, best)


def shards(tokens, router, price, w_in, w_out, assign):
    experts = router.shape[1]
    width = tokens.shape[1]
    local_tokens = tokens.shape[0]
    capacity = 3 * local_tokens // (2 * experts)
    dp_count = lax.axis_size("dp")
    first = w_in[0]
    second = w_out[0]
    affinity = jnp.dot(tokens, router, preferred_element_type=jnp.float32)
    onehot = assign[:, None] == jnp.arange(experts, dtype=jnp.int32)[None, :]
    own = jnp.sum(jnp.where(onehot, affinity, 0.0), axis=1)
    rival = jnp.max(jnp.where(onehot, -1e30, affinity - price[None, :]), axis=1)
    bid = own - rival + BID_STEP
    local_best = jnp.max(jnp.where(onehot, bid[:, None], -1e30), axis=0)
    lower = (jnp.arange(local_tokens)[:, None] >= jnp.arange(local_tokens)[None, :]).astype(jnp.bfloat16)
    running = jnp.dot(lower, onehot.astype(jnp.bfloat16), preferred_element_type=jnp.float32)
    slots = jnp.sum(jnp.where(onehot, running, 0.0), axis=1).astype(jnp.int32) - 1
    place = assign * capacity + slots
    pack = (place[None, :] == jnp.arange(experts * capacity, dtype=jnp.int32)[:, None]).astype(jnp.bfloat16)
    packed = jnp.dot(pack, tokens, preferred_element_type=jnp.float32).astype(jnp.bfloat16)
    best = jnp.full((8, 128), -1e30, jnp.float32).at[0, :experts].set(local_best)
    rows, bests = dispatch(packed.reshape(experts, capacity, width), best, dp_count)
    rows = rows.reshape(dp_count * experts * capacity, width)
    raw = jnp.dot(rows, first, preferred_element_type=jnp.float32)
    hidden = jax.nn.gelu(raw, approximate=True).astype(jnp.bfloat16)
    partial = jnp.dot(hidden, second, preferred_element_type=jnp.float32).astype(jnp.bfloat16)
    returned, all_bests = collect(
        partial.reshape(dp_count, experts, capacity, width), jnp.max(bests, axis=0)
    )
    new_price = jnp.max(all_bests, axis=0)[0, :experts]
    returned = returned.reshape(experts * capacity, width)
    picked = lax.dot_general(pack, returned, (((0,), (0,)), ((), ())), preferred_element_type=jnp.float32)
    gate = jax.nn.sigmoid(own)
    mixed = (gate[:, None] * picked).astype(jnp.bfloat16)
    return (mixed, new_price)


def solution(mesh):
    return jax.shard_map(
        shards,
        mesh=mesh,
        in_specs=(
            P(("dp", "expert"), None),
            P(),
            P(),
            P("expert", None, "dp"),
            P("expert", "dp", None),
            P(("dp", "expert")),
        ),
        out_specs=(P(("dp", "expert"), None), P()),
        check_vma=False,
    )
```

```python
import functools

import jax
import jax.numpy as jnp
from jax import lax
from jax.experimental import pallas as pl
from jax.experimental.pallas import tpu as pltpu
from jax.sharding import PartitionSpec as P

BID_STEP = 0.01
MESH = pl.DeviceIdType.MESH


def remote(src, dst, send, recv, a, b):
    return pltpu.make_async_remote_copy(
        src_ref=src, dst_ref=dst, send_sem=send, recv_sem=recv, device_id=(a, b), device_id_type=MESH
    )


def greet(dps, experts, a, b):
    barrier = pltpu.get_barrier_semaphore()
    for k in range(1, experts):
        pl.semaphore_signal(barrier, inc=1, device_id=(a, lax.rem(b + k, experts)), device_id_type=MESH)
    for k in range(1, dps):
        pl.semaphore_signal(barrier, inc=1, device_id=(lax.rem(a + k, dps), b), device_id_type=MESH)
    pl.semaphore_wait(barrier, experts + dps - 2)


def layer_kernel(
    dps, experts, packed, best, w_in, w_out, back, rows, bests, all_bests,
    win, wout, loaded, flat, hidden, part, pair, far, final, top,
    load_sem, own_sem, s1, r1, s2, r2, s3, r3, s4, r4, s5, r5, s6, r6, sb, rb, sd, rd,
):
    a, b = lax.axis_index("dp"), lax.axis_index("expert")
    nx, groups = dps // 2, experts // 2
    x, c = a // 2, lax.rem(a, 2)
    z, y = b // 2, lax.rem(b, 2)
    other = 2 * x + 1 - c
    capacity, width = packed.shape[1:]
    ff = win.shape[1]
    cut = 512
    tall = 2 * dps * capacity
    load_in = pltpu.make_async_copy(w_in, win, load_sem.at[0])
    load_out = pltpu.make_async_copy(w_out, wout, load_sem.at[1])
    load_in.start()
    greet(dps, experts, a, b)

    def ahead(k):
        return 2 * lax.rem(z + k // 2, groups) + lax.rem(y + k % 2, 2)

    def behind(k):
        return 2 * lax.rem(z + groups - k // 2, groups) + lax.rem(y + k % 2, 2)

    def xrow(q):
        return 2 * lax.rem(x + q, nx) + c

    def xback(q):
        return 2 * lax.rem(x + nx - q, nx) + c

    def out(k):
        e = ahead(k)
        return remote(packed.at[e], rows.at[k, a], s1.at[k], r1.at[k], a, e)

    def out_best(k):
        return remote(best, bests.at[k], sb.at[k], rb.at[k], a, ahead(k))

    def spread_best(k):
        return remote(top, all_bests.at[k], sd.at[k], rd.at[k], lax.rem(a + k, dps), b)

    def fan(q, k):
        return remote(rows.at[k, a], rows.at[k, a], s2.at[q - 1, k], r2.at[q - 1, k], xrow(q), b)

    def fan_in(q, k):
        row = xback(q)
        return remote(rows.at[k, row], rows.at[k, row], s2.at[q - 1, k], r2.at[q - 1, k], row, b)

    def share(q, k):
        row = xback(q)
        return remote(rows.at[k, row], rows.at[k, row], s3.at[q, k], r3.at[q, k], other, b)

    def share_in(q, k):
        row = xback(q) + 1 - 2 * c
        return remote(rows.at[k, row], rows.at[k, row], s3.at[q, k], r3.at[q, k], other, b)

    def beside(q, k):
        return remote(
            part.at[k, xrow(q) + 1 - 2 * c], pair.at[q, k], s4.at[q, k], r4.at[q, k], other, b
        )

    def across(q, k):
        return remote(pair.at[q, k], far.at[q - 1, k], s5.at[q - 1, k], r5.at[q - 1, k], xrow(q), b)

    def home(k):
        return remote(final.at[k], back.at[b], s6.at[k], r6.at[k], a, behind(k))

    own = pltpu.make_async_copy(packed.at[b], rows.at[0, a], own_sem.at[0])
    own_back = pltpu.make_async_copy(final.at[0], back.at[b], own_sem.at[2])

    def arrive(g):
        for k in (2 * g, 2 * g + 1):
            if k == 0:
                own.wait()
            else:
                out(k).wait_recv()
            for q in range(1, nx):
                fan(q, k).start()
            share(0, k).start()

    def forward(g):
        for k in (2 * g, 2 * g + 1):
            for q in range(1, nx):
                fan_in(q, k).wait_recv()
                share(q, k).start()

    def compute(g):
        for k in (2 * g, 2 * g + 1):
            for q in range(nx):
                share_in(q, k).wait_recv()
        load = pltpu.make_async_copy(rows.at[pl.ds(2 * g, 2)], loaded, own_sem.at[1])
        load.start()
        load.wait()

        def flatten(t, carry):
            cols = pl.ds(pl.multiple_of(t * cut, cut), cut)
            block = loaded[:, :, :, cols].astype(jnp.float32)
            flat[:, cols] = block.reshape(tall, cut).astype(jnp.bfloat16)
            return carry

        def first(t, carry):
            cols = pl.ds(pl.multiple_of(t * cut, cut), cut)
            raw = jnp.dot(flat[...], win[:, cols], preferred_element_type=jnp.float32)
            hidden[:, cols] = jax.nn.gelu(raw, approximate=True).astype(jnp.bfloat16)
            return carry

        def second(t, carry):
            cols = pl.ds(pl.multiple_of(t * cut, cut), cut)
            res = jnp.dot(hidden[...], wout[:, cols], preferred_element_type=jnp.float32)
            part[2 * g : 2 * g + 2, :, :, cols] = res.reshape(2, dps, capacity, cut).astype(jnp.bfloat16)
            return carry

        lax.fori_loop(0, width // cut, flatten, 0)
        if g == 0:
            load_in.wait()
        lax.fori_loop(0, ff // cut, first, 0)
        if g == 0:
            load_out.wait()
        lax.fori_loop(0, width // cut, second, 0)
        for q in list(range(1, nx)) + [0]:
            for k in (2 * g, 2 * g + 1):
                beside(q, k).start()

    def add_pair(g):
        for k in (2 * g, 2 * g + 1):
            for q in range(1, nx):
                beside(q, k).wait_recv()

                def add(t, carry):
                    cols = pl.ds(pl.multiple_of(t * cut, cut), cut)
                    total = part[k, xrow(q), :, cols].astype(jnp.float32)
                    total = total + pair[q, k, :, cols].astype(jnp.float32)
                    pair[q, k, :, cols] = total.astype(jnp.bfloat16)
                    return carry

                lax.fori_loop(0, width // cut, add, 0)
                across(q, k).start()

    def add_far(g):
        for k in (2 * g, 2 * g + 1):
            beside(0, k).wait_recv()
            for q in range(1, nx):
                across(q, k).wait_recv()

            def add(t, carry):
                cols = pl.ds(pl.multiple_of(t * cut, cut), cut)
                total = part[k, a, :, cols].astype(jnp.float32)
                total = total + pair[0, k, :, cols].astype(jnp.float32)
                for q in range(1, nx):
                    total = total + far[q - 1, k, :, cols].astype(jnp.float32)
                final[k, :, cols] = total.astype(jnp.bfloat16)
                return carry

            lax.fori_loop(0, width // cut, add, 0)
            if k == 0:
                own_back.start()
            else:
                home(k).start()

    own.start()
    for k in range(1, experts):
        out(k).start()
    for k in range(1, experts):
        out_best(k).start()
    load_out.start()
    arrive(0)
    arrive(1)
    forward(0)
    for g in range(groups):
        compute(g)
        if g + 2 < groups:
            arrive(g + 2)
        if g + 1 < groups:
            forward(g + 1)
        if g >= 1:
            add_pair(g - 1)
        if g >= 2:
            add_far(g - 2)
    add_pair(groups - 1)
    for k in range(1, experts):
        out_best(k).wait_recv()
    highest = best[...]
    for k in range(1, experts):
        highest = jnp.maximum(highest, bests[k])
    top[...] = highest
    all_bests[0] = highest
    for k in range(1, dps):
        spread_best(k).start()
    add_far(groups - 2)
    add_far(groups - 1)
    own_back.wait()
    for k in range(1, dps):
        spread_best(k).wait()
    for k in range(1, experts):
        e = ahead(k)
        remote(final.at[k], back.at[e], s6.at[k], r6.at[k], a, e).wait_recv()
        home(k).wait_send()
        out(k).wait_send()
        out_best(k).wait_send()
    for k in range(experts):
        for q in range(1, nx):
            fan(q, k).wait_send()
            across(q, k).wait_send()
        for q in range(nx):
            share(q, k).wait_send()
            beside(q, k).wait_send()


def layer(packed, best, w_in, w_out, dps):
    experts, capacity, width = packed.shape
    nx = dps // 2
    ff = w_in.shape[1]
    tall = 2 * dps * capacity
    dtype = packed.dtype
    sem = pltpu.SemaphoreType.DMA
    anywhere = pl.BlockSpec(memory_space=pl.ANY)
    inside = pl.BlockSpec(memory_space=pltpu.VMEM)
    return pl.pallas_call(
        functools.partial(layer_kernel, dps, experts),
        out_shape=(
            jax.ShapeDtypeStruct((experts, capacity, width), dtype),
            jax.ShapeDtypeStruct((experts, dps, capacity, width), dtype),
            jax.ShapeDtypeStruct((experts,) + best.shape, best.dtype),
            jax.ShapeDtypeStruct((dps,) + best.shape, best.dtype),
        ),
        in_specs=[anywhere, inside, anywhere, anywhere],
        out_specs=(anywhere, anywhere, inside, inside),
        scratch_shapes=[
            pltpu.VMEM((width, ff), dtype),
            pltpu.VMEM((ff, width), dtype),
            pltpu.VMEM((2, dps, capacity, width), dtype),
            pltpu.VMEM((tall, width), dtype),
            pltpu.VMEM((tall, ff), dtype),
            pltpu.VMEM((experts, dps, capacity, width), dtype),
            pltpu.VMEM((nx, experts, capacity, width), dtype),
            pltpu.VMEM((nx - 1, experts, capacity, width), dtype),
            pltpu.VMEM((experts, capacity, width), dtype),
            pltpu.VMEM(best.shape, best.dtype),
            sem((2,)),
            sem((3,)),
            sem((experts,)),
            sem((experts,)),
            sem((nx - 1, experts)),
            sem((nx - 1, experts)),
            sem((nx, experts)),
            sem((nx, experts)),
            sem((nx, experts)),
            sem((nx, experts)),
            sem((nx - 1, experts)),
            sem((nx - 1, experts)),
            sem((experts,)),
            sem((experts,)),
            sem((experts,)),
            sem((experts,)),
            sem((dps,)),
            sem((dps,)),
        ],
        compiler_params=pltpu.CompilerParams(
            collective_id=0, has_side_effects=True, vmem_limit_bytes=63 * 1024 * 1024
        ),
        name="layer",
    )(packed, best, w_in, w_out)


def shards(tokens, router, price, w_in, w_out, assign):
    experts = router.shape[1]
    width = tokens.shape[1]
    local_tokens = tokens.shape[0]
    capacity = -(-3 * local_tokens // (2 * experts * 8)) * 8
    dp_count = lax.axis_size("dp")
    first = w_in[0]
    second = w_out[0]
    affinity = jnp.dot(tokens, router, preferred_element_type=jnp.float32)
    onehot = assign[:, None] == jnp.arange(experts, dtype=jnp.int32)[None, :]
    own = jnp.sum(jnp.where(onehot, affinity, 0.0), axis=1)
    rival = jnp.max(jnp.where(onehot, -1e30, affinity - price[None, :]), axis=1)
    bid = own - rival + BID_STEP
    local_best = jnp.max(jnp.where(onehot, bid[:, None], -1e30), axis=0)
    lower = (jnp.arange(local_tokens)[:, None] >= jnp.arange(local_tokens)[None, :]).astype(jnp.bfloat16)
    running = jnp.dot(lower, onehot.astype(jnp.bfloat16), preferred_element_type=jnp.float32)
    slots = jnp.sum(jnp.where(onehot, running, 0.0), axis=1).astype(jnp.int32) - 1
    place = assign * capacity + slots
    pack = (place[None, :] == jnp.arange(experts * capacity, dtype=jnp.int32)[:, None]).astype(jnp.bfloat16)
    packed = jnp.dot(pack, tokens, preferred_element_type=jnp.float32).astype(jnp.bfloat16)
    best = jnp.full((8, 128), -1e30, jnp.float32).at[0, :experts].set(local_best)
    returned, _, _, all_bests = layer(
        packed.reshape(experts, capacity, width), best, first, second, dp_count
    )
    new_price = jnp.max(all_bests, axis=0)[0, :experts]
    returned = returned.reshape(experts * capacity, width)
    picked = lax.dot_general(pack, returned, (((0,), (0,)), ((), ())), preferred_element_type=jnp.float32)
    gate = jax.nn.sigmoid(own)
    mixed = (gate[:, None] * picked).astype(jnp.bfloat16)
    return (mixed, new_price)


def solution(mesh):
    return jax.shard_map(
        shards,
        mesh=mesh,
        in_specs=(
            P(("dp", "expert"), None),
            P(),
            P(),
            P("expert", None, "dp"),
            P("expert", "dp", None),
            P(("dp", "expert")),
        ),
        out_specs=(P(("dp", "expert"), None), P()),
        check_vma=False,
    )
```

```python
import functools

import jax
import jax.numpy as jnp
from jax import lax
from jax.experimental import pallas as pl
from jax.experimental.pallas import tpu as pltpu
from jax.sharding import PartitionSpec as P

BID_STEP = 0.01
MESH = pl.DeviceIdType.MESH


def remote(src, dst, send, recv, a, b):
    return pltpu.make_async_remote_copy(
        src_ref=src, dst_ref=dst, send_sem=send, recv_sem=recv, device_id=(a, b), device_id_type=MESH
    )


def greet(dps, experts, a, b):
    barrier = pltpu.get_barrier_semaphore()
    for k in range(1, experts):
        pl.semaphore_signal(barrier, inc=1, device_id=(a, lax.rem(b + k, experts)), device_id_type=MESH)
    for k in range(1, dps):
        pl.semaphore_signal(barrier, inc=1, device_id=(lax.rem(a + k, dps), b), device_id_type=MESH)
    pl.semaphore_wait(barrier, experts + dps - 2)


def layer_kernel(
    dps, experts, packed, best, w_in, w_out, back, rows, bests, all_bests,
    win, wout, loaded, flat, hidden, part, pair, far, final, top,
    load_sem, own_sem, s1, r1, s2, r2, s3, r3, s4, r4, s5, r5, s6, r6, sb, rb, sd, rd,
):
    a, b = lax.axis_index("dp"), lax.axis_index("expert")
    nx, groups = dps // 2, experts // 2
    x, c = a // 2, lax.rem(a, 2)
    z, y = b // 2, lax.rem(b, 2)
    other = 2 * x + 1 - c
    capacity, width = packed.shape[1:]
    ff = win.shape[1]
    cut = 512
    wide = 1024
    tall = 2 * dps * capacity
    load_in = pltpu.make_async_copy(w_in, win, load_sem.at[0])
    load_out = pltpu.make_async_copy(w_out, wout, load_sem.at[1])
    load_in.start()
    greet(dps, experts, a, b)

    order = list(range(groups))

    def behind(k):
        to = z
        for bit in range(groups.bit_length()):
            if order[k // 2] >> bit & 1:
                to = to + (1 - 2 * lax.rem(z // 2**bit, 2)) * 2**bit
        return 2 * to + lax.rem(y + k % 2, 2)

    ahead = behind

    def xrow(q):
        return 2 * lax.rem(x + q, nx) + c

    def xback(q):
        return 2 * lax.rem(x + nx - q, nx) + c

    def out(k):
        e = ahead(k)
        return remote(packed.at[e], rows.at[k, a], s1.at[k], r1.at[k], a, e)

    def out_best(k):
        return remote(best, bests.at[k], sb.at[k], rb.at[k], a, ahead(k))

    def spread_best(k):
        return remote(top, all_bests.at[k], sd.at[k], rd.at[k], lax.rem(a + k, dps), b)

    def fan(q, k):
        return remote(rows.at[k, a], rows.at[k, a], s2.at[q - 1, k], r2.at[q - 1, k], xrow(q), b)

    def fan_in(q, k):
        row = xback(q)
        return remote(rows.at[k, row], rows.at[k, row], s2.at[q - 1, k], r2.at[q - 1, k], row, b)

    def share(q, k):
        row = xback(q)
        return remote(rows.at[k, row], rows.at[k, row], s3.at[q, k], r3.at[q, k], other, b)

    def share_in(q, k):
        row = xback(q) + 1 - 2 * c
        return remote(rows.at[k, row], rows.at[k, row], s3.at[q, k], r3.at[q, k], other, b)

    def beside(q, k):
        return remote(
            part.at[k, xrow(q) + 1 - 2 * c], pair.at[q, k], s4.at[q, k], r4.at[q, k], other, b
        )

    def across(q, k):
        return remote(pair.at[q, k], far.at[q - 1, k], s5.at[q - 1, k], r5.at[q - 1, k], xrow(q), b)

    def home(k):
        return remote(final.at[k], back.at[b], s6.at[k], r6.at[k], a, behind(k))

    own = pltpu.make_async_copy(packed.at[b], rows.at[0, a], own_sem.at[0])
    own_back = pltpu.make_async_copy(final.at[0], back.at[b], own_sem.at[2])

    def arrive(g):
        for k in (2 * g, 2 * g + 1):
            if k == 0:
                own.wait()
            else:
                out(k).wait_recv()
            for q in range(1, nx):
                fan(q, k).start()
            share(0, k).start()

    def forward(g):
        for k in (2 * g, 2 * g + 1):
            for q in range(1, nx):
                fan_in(q, k).wait_recv()
                share(q, k).start()

    def compute(g):
        for k in (2 * g, 2 * g + 1):
            for q in range(nx):
                share_in(q, k).wait_recv()
        load = pltpu.make_async_copy(rows.at[pl.ds(2 * g, 2)], loaded, own_sem.at[1])
        load.start()
        load.wait()

        def flatten(t, carry):
            cols = pl.ds(pl.multiple_of(t * cut, cut), cut)
            block = loaded[:, :, :, cols].astype(jnp.float32)
            flat[:, cols] = block.reshape(tall, cut).astype(jnp.bfloat16)
            return carry

        def first(t, carry):
            cols = pl.ds(pl.multiple_of(t * wide, wide), wide)
            raw = jnp.dot(flat[...], win[:, cols], preferred_element_type=jnp.float32)
            hidden[:, cols] = jax.nn.gelu(raw, approximate=True).astype(jnp.bfloat16)
            return carry

        def second(t, carry):
            cols = pl.ds(pl.multiple_of(t * wide, wide), wide)
            res = jnp.dot(hidden[...], wout[:, cols], preferred_element_type=jnp.float32)
            part[2 * g : 2 * g + 2, :, :, cols] = res.reshape(2, dps, capacity, wide).astype(jnp.bfloat16)
            return carry

        lax.fori_loop(0, width // cut, flatten, 0)
        if g == 0:
            load_in.wait()
        lax.fori_loop(0, ff // wide, first, 0)
        if g + 2 < groups:
            arrive(g + 2)
        if g + 1 < groups:
            forward(g + 1)
        if g >= 1:
            add_pair(g - 1)
        if g >= 2:
            add_far(g - 2)
        if g == 0:
            load_out.wait()
        lax.fori_loop(0, width // wide, second, 0)
        for q in list(range(1, nx)) + [0]:
            for k in (2 * g, 2 * g + 1):
                beside(q, k).start()

    def add_pair(g):
        for k in (2 * g, 2 * g + 1):
            for q in range(1, nx):
                beside(q, k).wait_recv()

                def add(t, carry):
                    cols = pl.ds(pl.multiple_of(t * cut, cut), cut)
                    total = part[k, xrow(q), :, cols].astype(jnp.float32)
                    total = total + pair[q, k, :, cols].astype(jnp.float32)
                    pair[q, k, :, cols] = total.astype(jnp.bfloat16)
                    return carry

                lax.fori_loop(0, width // cut, add, 0)
                across(q, k).start()

    def add_far(g):
        for k in (2 * g, 2 * g + 1):
            beside(0, k).wait_recv()
            for q in range(1, nx):
                across(q, k).wait_recv()

            def add(t, carry):
                cols = pl.ds(pl.multiple_of(t * cut, cut), cut)
                total = part[k, a, :, cols].astype(jnp.float32)
                total = total + pair[0, k, :, cols].astype(jnp.float32)
                for q in range(1, nx):
                    total = total + far[q - 1, k, :, cols].astype(jnp.float32)
                final[k, :, cols] = total.astype(jnp.bfloat16)
                return carry

            lax.fori_loop(0, width // cut, add, 0)
            if k == 0:
                own_back.start()
            else:
                home(k).start()

    own.start()
    for k in range(1, experts):
        out(k).start()
    for k in range(1, experts):
        out_best(k).start()
    load_out.start()
    arrive(0)
    arrive(1)
    forward(0)
    for g in range(groups):
        compute(g)
    add_pair(groups - 1)
    for k in range(1, experts):
        out_best(k).wait_recv()
    highest = best[...]
    for k in range(1, experts):
        highest = jnp.maximum(highest, bests[k])
    top[...] = highest
    all_bests[0] = highest
    for k in range(1, dps):
        spread_best(k).start()
    add_far(groups - 2)
    add_far(groups - 1)
    own_back.wait()
    for k in range(1, dps):
        spread_best(k).wait()
    for k in range(1, experts):
        e = ahead(k)
        remote(final.at[k], back.at[e], s6.at[k], r6.at[k], a, e).wait_recv()
        home(k).wait_send()
        out(k).wait_send()
        out_best(k).wait_send()
    for k in range(experts):
        for q in range(1, nx):
            fan(q, k).wait_send()
            across(q, k).wait_send()
        for q in range(nx):
            share(q, k).wait_send()
            beside(q, k).wait_send()


def layer(packed, best, w_in, w_out, dps):
    experts, capacity, width = packed.shape
    nx = dps // 2
    ff = w_in.shape[1]
    tall = 2 * dps * capacity
    dtype = packed.dtype
    sem = pltpu.SemaphoreType.DMA
    anywhere = pl.BlockSpec(memory_space=pl.ANY)
    inside = pl.BlockSpec(memory_space=pltpu.VMEM)
    return pl.pallas_call(
        functools.partial(layer_kernel, dps, experts),
        out_shape=(
            jax.ShapeDtypeStruct((experts, capacity, width), dtype),
            jax.ShapeDtypeStruct((experts, dps, capacity, width), dtype),
            jax.ShapeDtypeStruct((experts,) + best.shape, best.dtype),
            jax.ShapeDtypeStruct((dps,) + best.shape, best.dtype),
        ),
        in_specs=[anywhere, inside, anywhere, anywhere],
        out_specs=(anywhere, anywhere, inside, inside),
        scratch_shapes=[
            pltpu.VMEM((width, ff), dtype),
            pltpu.VMEM((ff, width), dtype),
            pltpu.VMEM((2, dps, capacity, width), dtype),
            pltpu.VMEM((tall, width), dtype),
            pltpu.VMEM((tall, ff), dtype),
            pltpu.VMEM((experts, dps, capacity, width), dtype),
            pltpu.VMEM((nx, experts, capacity, width), dtype),
            pltpu.VMEM((nx - 1, experts, capacity, width), dtype),
            pltpu.VMEM((experts, capacity, width), dtype),
            pltpu.VMEM(best.shape, best.dtype),
            sem((2,)),
            sem((3,)),
            sem((experts,)),
            sem((experts,)),
            sem((nx - 1, experts)),
            sem((nx - 1, experts)),
            sem((nx, experts)),
            sem((nx, experts)),
            sem((nx, experts)),
            sem((nx, experts)),
            sem((nx - 1, experts)),
            sem((nx - 1, experts)),
            sem((experts,)),
            sem((experts,)),
            sem((experts,)),
            sem((experts,)),
            sem((dps,)),
            sem((dps,)),
        ],
        compiler_params=pltpu.CompilerParams(
            collective_id=0, has_side_effects=True, vmem_limit_bytes=63 * 1024 * 1024
        ),
        name="layer",
    )(packed, best, w_in, w_out)


def shards(tokens, router, price, w_in, w_out, assign):
    experts = router.shape[1]
    width = tokens.shape[1]
    local_tokens = tokens.shape[0]
    capacity = -(-3 * local_tokens // (2 * experts * 8)) * 8
    dp_count = lax.axis_size("dp")
    first = w_in[0]
    second = w_out[0]
    affinity = jnp.dot(tokens, router, preferred_element_type=jnp.float32)
    onehot = assign[:, None] == jnp.arange(experts, dtype=jnp.int32)[None, :]
    own = jnp.sum(jnp.where(onehot, affinity, 0.0), axis=1)
    rival = jnp.max(jnp.where(onehot, -1e30, affinity - price[None, :]), axis=1)
    bid = own - rival + BID_STEP
    local_best = jnp.max(jnp.where(onehot, bid[:, None], -1e30), axis=0)
    lower = (jnp.arange(local_tokens)[:, None] >= jnp.arange(local_tokens)[None, :]).astype(jnp.bfloat16)
    running = jnp.dot(lower, onehot.astype(jnp.bfloat16), preferred_element_type=jnp.float32)
    slots = jnp.sum(jnp.where(onehot, running, 0.0), axis=1).astype(jnp.int32) - 1
    place = assign * capacity + slots
    pack = (place[None, :] == jnp.arange(experts * capacity, dtype=jnp.int32)[:, None]).astype(jnp.bfloat16)
    packed = jnp.dot(pack, tokens, preferred_element_type=jnp.float32).astype(jnp.bfloat16)
    best = jnp.full((8, 128), -1e30, jnp.float32).at[0, :experts].set(local_best)
    returned, _, _, all_bests = layer(
        packed.reshape(experts, capacity, width), best, first, second, dp_count
    )
    new_price = jnp.max(all_bests, axis=0)[0, :experts]
    returned = returned.reshape(experts * capacity, width)
    picked = lax.dot_general(pack, returned, (((0,), (0,)), ((), ())), preferred_element_type=jnp.float32)
    gate = jax.nn.sigmoid(own)
    mixed = (gate[:, None] * picked).astype(jnp.bfloat16)
    return (mixed, new_price)


def solution(mesh):
    return jax.shard_map(
        shards,
        mesh=mesh,
        in_specs=(
            P(("dp", "expert"), None),
            P(),
            P(),
            P("expert", None, "dp"),
            P("expert", "dp", None),
            P(("dp", "expert")),
        ),
        out_specs=(P(("dp", "expert"), None), P()),
        check_vma=False,
    )
```
